32 devices in a mesh: space: 4 (over x, core), orient: 8 (over z, y).
Axes of the slice: x: 2, y: 2, z: 4, core: 2. Of those that a mesh axis runs over, the one named last changes fastest.
Arguments:
- q_init: bfloat16 [256, 64, 128, 128], P('orient', 'space'), may hold values from 0.5 to 1.5
- partner: bfloat16 [256, 64, 128, 128], P('orient', 'space'), may hold values from 0.5 to 1.5
- field: bfloat16 [6, 64, 128, 128], P(None, 'space'), may hold values from -3 to 3
- orientations: float32 [3, 256], replicated, may hold values from -1 to 1, as said below
- orient_weight: float32 [256], replicated, may hold values from 0.03 to 0.12
- rotation: bfloat16 [256, 256], replicated, may hold values from -1 to 1
Outputs:
- q_final: bfloat16 [256, 64, 128, 128], P('orient', 'space')
- new_field: float32 [6, 64, 128, 128], P(None, 'space', 'orient')
The draws below stay inside these ranges and needn't reach their ends.
Inputs may be any that keep to these rules, and one draw needn't show every extreme that they name: `orientations`: each column is a unit vector.
All inputs are finite; a program needn't handle non-finite values.
Results may differ from the reference program's by a relative error of at most 0.0057.
Values may be sent and summed in bfloat16 or wider, within the bound.
No kernel may reach another device: no remote copies, remote signals or barrier semaphores. Data moves between devices by JAX's collectives and lax.ppermute only.
A program may use at most 320 MiB of HBM per device.

```python
import math
import jax
import jax.numpy as jnp
from jax import lax

NO = 256
NX = 128
NY = 128
STEPS = 2
NZ = 64


def draw_orientations(key, part):
    raw = jax.random.normal(key, (3, NO), jnp.float32)
    return raw / jnp.sqrt(jnp.sum(raw * raw, axis=0, keepdims=True))


def draw_rotation(key, part):
    spread = jax.random.normal(key, (NO, NO), jnp.float32)
    spread = jnp.clip(spread, -4.0, 4.0)
    return (0.6 * jnp.eye(NO, dtype=jnp.float32) + 0.4 * spread / jnp.sqrt(NO * 1.0)).astype(jnp.bfloat16)


def block_levels(stream_key, dims, pieces, low, high):
    def one(position, blocks):
        draws = jax.random.uniform(jax.random.fold_in(jax.random.fold_in(stream_key, 6), position), (blocks,), jnp.float32, low / len(pieces), high / len(pieces))
        return jnp.repeat(jnp.exp(draws), dims[position] // blocks).reshape((-1,) + (1,) * (len(dims) - position - 1))

    gain = one(*pieces[0])
    for cut in pieces[1:]:
        gain = gain * one(*cut)
    return gain


def centred(key, shape, width, bound, shards=(), kind=jnp.bfloat16):
    loudness = block_levels(key, shape, shards, -0.22, 0.18) if shards else 1.0
    values = jax.random.normal(key, shape, jnp.float32) * width * loudness
    return jnp.minimum(jnp.maximum(values, -bound), bound).astype(kind)


def setup_inputs(seed: int = 0) -> dict:
    streams_of = jax.random.split(jax.random.key(seed), 7)
    return {
        "q_init": jnp.clip(0.5 + 1.0 * jax.random.uniform(streams_of[0], (NO, NZ, NY, NX), jnp.float32) ** block_levels(streams_of[0], (NO, NZ, NY, NX), ((0, 8), (1, 4)), -0.2, 0.2), 0.5, 1.5).astype(jnp.bfloat16),
        "partner": jnp.clip(0.5 + 1.0 * jax.random.uniform(streams_of[1], (NO, NZ, NY, NX), jnp.float32) ** block_levels(streams_of[1], (NO, NZ, NY, NX), ((0, 8), (1, 4)), -0.2, 0.2), 0.5, 1.5).astype(jnp.bfloat16),
        "field": centred(streams_of[2], (6, NZ, NY, NX), 0.5, 3.0, ((1, 4),)),
        "orientations": draw_orientations(jax.random.fold_in(streams_of[6], 71), 0),
        "orient_weight": jnp.clip(jnp.exp(jax.random.uniform(streams_of[4], (NO,), jnp.float32, math.log(0.03), math.log(0.12))), 0.03, 0.12),
        "rotation": draw_rotation(jax.random.fold_in(streams_of[6], 71), 0),
    }


step_length = 0.3
relax_rate = 0.5
coupling = 8.0


def angle_tables(orientations):
    along_x = orientations[0]
    along_y = orientations[1]
    along_z = orientations[2]
    field_terms = jnp.stack([along_x * along_x, along_y * along_y, along_z * along_z, 2.0 * along_x * along_y, 2.0 * along_x * along_z, 2.0 * along_y * along_z])
    tensor_terms = jnp.stack([along_x * along_x - 1.0 / 3.0, along_y * along_y - 1.0 / 3.0, along_z * along_z - 1.0 / 3.0, along_x * along_y, along_x * along_z, along_y * along_z])
    return field_terms, tensor_terms


def upwind(center, below, above, speeds):
    speed_x, speed_y, speed_z = speeds
    back_x = center - jnp.roll(center, 1, axis=-1)
    fore_x = jnp.roll(center, -1, axis=-1) - center
    back_y = center - jnp.roll(center, 1, axis=-2)
    fore_y = jnp.roll(center, -1, axis=-2) - center
    back_z = center - below
    fore_z = above - center
    total = jnp.maximum(speed_x, 0.0) * back_x + jnp.minimum(speed_x, 0.0) * fore_x
    total = total + jnp.maximum(speed_y, 0.0) * back_y + jnp.minimum(speed_y, 0.0) * fore_y
    total = total + jnp.maximum(speed_z, 0.0) * back_z + jnp.minimum(speed_z, 0.0) * fore_z
    return center - step_length * total


def reference(q_init, partner, field, orientations, orient_weight, rotation):
    field_terms, tensor_terms = angle_tables(orientations)
    wide_field = field.astype(jnp.float32)

    def advect_one(inputs):
        block, speeds, terms = inputs
        center = block.astype(jnp.float32)
        below = jnp.roll(center, 1, axis=0)
        above = jnp.roll(center, -1, axis=0)
        moved = upwind(center, below, above, (speeds[0], speeds[1], speeds[2]))
        potential = jnp.tensordot(terms, wide_field, axes=1, precision=lax.Precision.HIGHEST)
        return (moved * jnp.exp(-step_length * potential)).astype(jnp.bfloat16)

    def rotate_slice(layer):
        flat = layer.reshape(layer.shape[0], -1)
        return jnp.dot(rotation, flat, preferred_element_type=jnp.float32).astype(jnp.bfloat16).reshape(layer.shape)

    state = q_init
    for contour in range(STEPS):
        advected = lax.map(advect_one, (state, orientations.T, field_terms.T))
        turned = lax.map(rotate_slice, jnp.moveaxis(advected, 1, 0))
        state = jnp.moveaxis(turned, 0, 1)

    all_terms = tensor_terms * orient_weight[None, :]

    def tensor_slice(inputs):
        layer, other = inputs
        product = layer.astype(jnp.float32) * other.astype(jnp.float32)
        sums = jnp.dot(all_terms, product.reshape(product.shape[0], -1), precision=lax.Precision.HIGHEST)
        return sums.reshape((6,) + product.shape[1:])

    tensor = lax.map(tensor_slice, (jnp.moveaxis(state, 1, 0), jnp.moveaxis(partner, 1, 0)))
    tensor = jnp.moveaxis(tensor, 0, 1)
    new_field = (1.0 - relax_rate) * wide_field + relax_rate * coupling * tensor
    return state, new_field
```

```python
import functools

import jax
import jax.numpy as jnp
from jax import lax
from jax.experimental import pallas as pl
from jax.experimental.pallas import tpu as pltpu
from jax.sharding import PartitionSpec as P

SHARES = (3, 3, 8, 2)

step_length = 0.3
relax_rate = 0.5
coupling = 8.0


F32 = jnp.float32
BF16 = jnp.bfloat16


def ring(count, shift):
    return [(i, (i + shift) % count) for i in range(count)]


def angle_tables(orientations):
    along_x = orientations[0]
    along_y = orientations[1]
    along_z = orientations[2]
    field_terms = jnp.stack(
        [
            along_x * along_x,
            along_y * along_y,
            along_z * along_z,
            2.0 * along_x * along_y,
            2.0 * along_x * along_z,
            2.0 * along_y * along_z,
        ]
    )
    tensor_terms = jnp.stack(
        [
            along_x * along_x - 1.0 / 3.0,
            along_y * along_y - 1.0 / 3.0,
            along_z * along_z - 1.0 / 3.0,
            along_x * along_y,
            along_x * along_z,
            along_y * along_z,
        ]
    )
    return (field_terms, tensor_terms)


def stencil_weights(orientations):
    low = step_length * jnp.maximum(orientations, 0.0)
    high = -step_length * jnp.minimum(orientations, 0.0)
    middle = 1.0 - jnp.sum(low + high, axis=0)
    return jnp.stack([low[0], high[0], low[1], high[1], low[2], high[2], middle])


def advect_kernel(has_low, has_high, *refs):
    refs = list(refs)
    coef, below, centre, above = refs[:4]
    rest = refs[4:]
    low = rest.pop(0) if has_low else None
    high = rest.pop(0) if has_high else None
    field, out, staged = rest
    z = pl.program_id(0)
    last = pl.num_programs(0) - 1
    count, width = staged.shape[0], staged.shape[1]
    owners, rows = out.shape[0], out.shape[2]

    def one(o, carry):
        f = centre[o, 0].astype(F32)
        zm = below[o, 0].astype(F32)
        if has_low:
            zm = jnp.where(z == 0, low[o, 0].astype(F32), zm)
        zp = above[o, 0].astype(F32)
        if has_high:
            zp = jnp.where(z == last, high[o, 0].astype(F32), zp)
        lanes = f.shape[1]
        moved = coef[6, o] * f
        moved += coef[0, o] * pltpu.roll(f, 1, 1) + coef[1, o] * pltpu.roll(f, lanes - 1, 1)
        moved += coef[2, o] * pltpu.roll(f, 1, 0) + coef[3, o] * pltpu.roll(f, width - 1, 0)
        moved += coef[4, o] * zm + coef[5, o] * zp
        exponent = coef[7, o] * field[0, 0].astype(F32)
        for c in range(1, 6):
            exponent += coef[7 + c, o] * field[c, 0].astype(F32)
        staged[o] = moved * jnp.exp(exponent)
        return carry

    lax.fori_loop(0, count, one, 0)
    for owner in range(owners):
        part = staged[:, owner * rows : (owner + 1) * rows, :]
        out[owner, 0] = jnp.swapaxes(part, 0, 1).astype(BF16)


def advect(coef, q, low, high, field, start, depth, owners):
    count, layers, width, lanes = q.shape
    rows = width // owners
    block = (count, 1, width, lanes)
    in_specs = [
        pl.BlockSpec(memory_space=pltpu.SMEM),
        pl.BlockSpec(block, lambda z: (0, jnp.maximum(start + z - 1, 0), 0, 0)),
        pl.BlockSpec(block, lambda z: (0, start + z, 0, 0)),
        pl.BlockSpec(block, lambda z: (0, jnp.minimum(start + z + 1, layers - 1), 0, 0)),
    ]
    operands = [coef, q, q, q]
    for halo in (low, high):
        if halo is not None:
            in_specs.append(pl.BlockSpec(block, lambda z: (0, 0, 0, 0)))
            operands.append(halo)
    in_specs.append(pl.BlockSpec((6, 1, width, lanes), lambda z: (0, start + z, 0, 0)))
    operands.append(field)
    cells = count * depth * width * lanes
    return pl.pallas_call(
        functools.partial(advect_kernel, low is not None, high is not None),
        grid=(depth,),
        in_specs=in_specs,
        out_specs=pl.BlockSpec((owners, 1, rows, count, lanes), lambda z: (0, z, 0, 0, 0)),
        out_shape=jax.ShapeDtypeStruct((owners, depth, rows, count, lanes), BF16),
        scratch_shapes=[pltpu.VMEM((count, width, lanes), F32)],
        cost_estimate=pl.CostEstimate(
            flops=30 * cells, transcendentals=cells, bytes_accessed=8 * cells
        ),
        name="advect_first",
    )(*operands)


def turn_kernel(rotation, block, out):
    owners, rows, count, lanes = block.shape[0], block.shape[2], block.shape[3], block.shape[4]
    total = owners * count
    pair = 2 if rows % 2 == 0 else 1

    def one(step, carry):
        columns = []
        for j in range(pair):
            y = step * pair + j
            columns.append(block[:, 0, y].astype(F32).reshape(total, lanes).astype(BF16))
        wide = jnp.concatenate(columns, axis=1) if pair > 1 else columns[0]
        turned = jnp.dot(rotation[...], wide, preferred_element_type=F32).astype(BF16)
        for j in range(pair):
            out[0, step * pair + j] = turned[:, j * lanes : (j + 1) * lanes]
        return carry

    lax.fori_loop(0, rows // pair, one, 0)


def turn(rotation, block):
    owners, depth, rows, count, lanes = block.shape
    total = owners * count
    cells = total * depth * rows * lanes
    return pl.pallas_call(
        turn_kernel,
        grid=(depth,),
        in_specs=[
            pl.BlockSpec((total, total), lambda z: (0, 0)),
            pl.BlockSpec((owners, 1, rows, count, lanes), lambda z: (0, z, 0, 0, 0)),
        ],
        out_specs=pl.BlockSpec((1, rows, total, lanes), lambda z: (z, 0, 0, 0)),
        out_shape=jax.ShapeDtypeStruct((depth, rows, total, lanes), BF16),
        cost_estimate=pl.CostEstimate(
            flops=2 * total * cells, transcendentals=0, bytes_accessed=4 * cells
        ),
        name="turn_first",
    )(rotation, block)


def advect_turn_kernel(
    rotation, weights, terms, below, centre, above, low, high, south, north, field, out, mixed, powers
):
    z = pl.program_id(0)
    last = pl.num_programs(0) - 1
    rows, total, lanes = centre.shape[1:]
    owners, count = out.shape[0], out.shape[3]
    pair = 2 if rows % 2 == 0 else 1
    piece = 64 if total % 64 == 0 else total

    def one(step, carry):
        for j in range(pair):
            y = step * pair + j
            powers[...] = jnp.dot(terms[...], field[0, y], preferred_element_type=F32)
            for base in range(0, total, piece):
                part = pl.ds(base, piece)
                f = centre[0, y, part].astype(F32)
                ym = centre[0, jnp.maximum(y - 1, 0), part].astype(F32)
                ym = jnp.where(y == 0, south[0, 0, part].astype(F32), ym)
                yp = centre[0, jnp.minimum(y + 1, rows - 1), part].astype(F32)
                yp = jnp.where(y == rows - 1, north[0, 0, part].astype(F32), yp)
                zm = below[0, y, part].astype(F32)
                zm = jnp.where(z == 0, low[0, y, part].astype(F32), zm)
                zp = above[0, y, part].astype(F32)
                zp = jnp.where(z == last, high[0, y, part].astype(F32), zp)
                moved = weights[6, part] * f
                moved += weights[0, part] * pltpu.roll(f, 1, 1)
                moved += weights[1, part] * pltpu.roll(f, lanes - 1, 1)
                moved += weights[2, part] * ym + weights[3, part] * yp
                moved += weights[4, part] * zm + weights[5, part] * zp
                mixed[part, j * lanes : (j + 1) * lanes] = (
                    moved * jnp.exp(powers[part])
                ).astype(BF16)
        turned = jnp.dot(rotation[...], mixed[...], preferred_element_type=F32)
        for j in range(pair):
            column = turned[:, j * lanes : (j + 1) * lanes]
            out[:, 0, step * pair + j] = column.reshape(owners, count, lanes).astype(BF16)
        return carry

    lax.fori_loop(0, rows // pair, one, 0)


def advect_turn(rotation, weights, terms, state, low, high, south, north, field, owners):
    depth, rows, total, lanes = state.shape
    count = total // owners
    layer = (1, rows, total, lanes)
    edge = (1, 1, total, lanes)
    pair = 2 if rows % 2 == 0 else 1
    cells = total * depth * rows * lanes
    fixed = lambda z: (0, 0, 0, 0)
    here = lambda z: (z, 0, 0, 0)
    return pl.pallas_call(
        advect_turn_kernel,
        grid=(depth,),
        in_specs=[
            pl.BlockSpec((total, total), lambda z: (0, 0)),
            pl.BlockSpec(weights.shape, lambda z: (0, 0, 0)),
            pl.BlockSpec(terms.shape, lambda z: (0, 0)),
            pl.BlockSpec(layer, lambda z: (jnp.maximum(z - 1, 0), 0, 0, 0)),
            pl.BlockSpec(layer, here),
            pl.BlockSpec(layer, lambda z: (jnp.minimum(z + 1, depth - 1), 0, 0, 0)),
            pl.BlockSpec(layer, fixed),
            pl.BlockSpec(layer, fixed),
            pl.BlockSpec(edge, here),
            pl.BlockSpec(edge, here),
            pl.BlockSpec((1,) + field.shape[1:], here),
        ],
        out_specs=pl.BlockSpec((owners, 1, rows, count, lanes), lambda z: (0, z, 0, 0, 0)),
        out_shape=jax.ShapeDtypeStruct((owners, depth, rows, count, lanes), BF16),
        scratch_shapes=[
            pltpu.VMEM((total, pair * lanes), BF16),
            pltpu.VMEM((total, lanes), F32),
        ],
        cost_estimate=pl.CostEstimate(
            flops=2 * total * cells, transcendentals=cells, bytes_accessed=8 * cells
        ),
        name="advect_turn",
    )(rotation, weights, terms, state, state, state, low, high, south, north, field)


def gather_kernel(*refs):
    coef, block, partner = refs[:3]
    state, partial = refs[-2:]
    owners, rows, count = block.shape[0], block.shape[2], block.shape[3]
    for owner in range(owners):
        part = pl.ds(owner * rows, rows)
        mine = jnp.swapaxes(block[owner, 0].astype(F32), 0, 1)
        state[:, 0, part, :] = mine.astype(BF16)
        sums = [None] * 6
        for o in range(count):
            product = mine[o] * partner[o, 0, part, :].astype(F32)
            for c in range(6):
                term = coef[c, o] * product
                sums[c] = term if sums[c] is None else sums[c] + term
        for c in range(6):
            partial[owner, c, 0] = sums[c].astype(partial.dtype)


def gather(coef, block, partner, state, start, kind):
    owners, depth, rows, count, lanes = block.shape
    width = partner.shape[2]
    cells = owners * depth * rows * count * lanes
    slab = pl.BlockSpec((count, 1, width, lanes), lambda z: (0, start + z, 0, 0))
    operands = [coef, block, partner]
    in_specs = [
        pl.BlockSpec(memory_space=pltpu.SMEM),
        pl.BlockSpec((owners, 1, rows, count, lanes), lambda z: (0, z, 0, 0, 0)),
        slab,
    ]
    aliases = {}
    if state is not None:
        aliases = {3: 0}
        operands.append(state)
        in_specs.append(pl.BlockSpec(memory_space=pl.ANY))
    return pl.pallas_call(
        gather_kernel,
        grid=(depth,),
        in_specs=in_specs,
        out_specs=[
            slab,
            pl.BlockSpec((owners, 6, 1, rows, lanes), lambda z: (0, 0, z, 0, 0)),
        ],
        out_shape=[
            jax.ShapeDtypeStruct(partner.shape, BF16),
            jax.ShapeDtypeStruct((owners, 6, depth, rows, lanes), kind),
        ],
        input_output_aliases=aliases,
        cost_estimate=pl.CostEstimate(
            flops=14 * cells, transcendentals=0, bytes_accessed=6 * cells
        ),
        name="gather_last",
    )(*operands)


def exchange(block):
    return lax.all_to_all(block, "orient", split_axis=0, concat_axis=0, tiled=True)


def halve(block):
    owners = lax.axis_size("orient")
    me = lax.axis_index("orient")
    rest = block.shape[1:]
    stride = 1
    held = block
    kept = owners
    while kept > 1:
        bit = (me // stride) % 2
        pairs = held.reshape((kept // 2, 2) + rest)
        mine = lax.dynamic_index_in_dim(pairs, bit, 1, keepdims=False)
        theirs = lax.dynamic_index_in_dim(pairs, 1 - bit, 1, keepdims=False)
        if kept == 2:
            theirs = theirs.astype(BF16)
        came = lax.ppermute(theirs, "orient", [(i, i ^ stride) for i in range(owners)])
        held = mine.astype(F32) + came.astype(F32)
        kept //= 2
        stride *= 2
    return held[0]


def chunk_sizes(layers):
    whole = sum(SHARES)
    sizes = [max(1, layers * share // whole) for share in SHARES]
    sizes[2] += layers - sum(sizes)
    return sizes


def staged_device(q_init, partner, field, orientations, orient_weight, rotation):
    owners = lax.axis_size("orient")
    slabs = lax.axis_size("space")
    me = lax.axis_index("orient")
    count, layers, width, lanes = q_init.shape
    rows = width // owners
    sizes = chunk_sizes(layers)
    chunks = len(sizes)
    starts = [sum(sizes[:c]) for c in range(chunks)]

    first = lax.ppermute(q_init[:, layers - 1 :], "space", ring(slabs, 1))
    final = lax.ppermute(q_init[:, :1], "space", ring(slabs, -1))

    field_terms, tensor_terms = angle_tables(orientations)
    weights = stencil_weights(orientations)
    exponent_terms = -step_length * field_terms
    local_coef = lax.dynamic_slice_in_dim(
        jnp.concatenate([weights, exponent_terms]), me * count, count, 1
    )
    local_tensor = lax.dynamic_slice_in_dim(
        tensor_terms * orient_weight[None, :], me * count, count, 1
    )
    wide_weights = jnp.broadcast_to(weights[:, :, None], weights.shape + (lanes,))
    top = lax.reduce_precision(exponent_terms, 8, 7)
    left = exponent_terms - top
    centre = lax.reduce_precision(left, 8, 7)
    split_terms = jnp.concatenate([top, centre, left - centre]).astype(BF16).T
    own_field = lax.dynamic_slice_in_dim(field, me * rows, rows, 2)
    row_field = jnp.transpose(own_field, (1, 2, 0, 3))
    row_field = jnp.concatenate([row_field] * 3, axis=2)
    padding = 32 - split_terms.shape[1]
    split_terms = jnp.pad(split_terms, ((0, 0), (0, padding)))
    row_field = jnp.pad(row_field, ((0, 0), (0, 0), (0, padding), (0, 0)))

    turned = {}
    souths = {}
    norths = {}
    for c in ORDER:
        sent = advect(
            local_coef,
            q_init,
            first if c == 0 else None,
            final if c == chunks - 1 else None,
            field,
            starts[c],
            sizes[c],
            owners,
        )
        got = exchange(sent)
        turned[c] = turn(rotation, got)
        souths[c] = lax.ppermute(turned[c][:, rows - 1 :], "orient", ring(owners, 1))
        norths[c] = lax.ppermute(turned[c][:, :1], "orient", ring(owners, -1))
    under = lax.ppermute(turned[chunks - 1][-1:], "space", ring(slabs, 1))
    over = lax.ppermute(turned[0][:1], "space", ring(slabs, -1))

    state = None
    sums = {}
    for c in ORDER:
        low = under if c == 0 else turned[c - 1][-1:]
        high = over if c == chunks - 1 else turned[c + 1][:1]
        sent = advect_turn(
            rotation,
            wide_weights,
            split_terms,
            turned[c],
            low,
            high,
            souths[c],
            norths[c],
            row_field[starts[c] : starts[c] + sizes[c]],
            owners,
        )
        got = exchange(sent)
        closing = c == ORDER[-1]
        state, partial = gather(
            local_tensor, got, partner, state, starts[c], BF16 if closing else F32
        )
        if closing or owners & (owners - 1):
            sums[c] = jnp.sum(exchange(partial).astype(F32), axis=0)
        else:
            sums[c] = halve(partial)
    tensor = jnp.concatenate([sums[c] for c in range(chunks)], axis=1)
    new_field = (1.0 - relax_rate) * own_field.astype(F32) + relax_rate * coupling * tensor
    return (state, new_field)


ORDER = (1, 2, 0, 3)


def solution(mesh):
    in_specs = (
        P("orient", "space", None, None),
        P("orient", "space", None, None),
        P(None, "space", None, None),
        P(),
        P(),
        P(),
    )
    out_specs = (P("orient", "space", None, None), P(None, "space", "orient", None))
    return jax.shard_map(
        staged_device, mesh=mesh, in_specs=in_specs, out_specs=out_specs, check_vma=False
    )
```

```python
import functools

import jax
import jax.numpy as jnp
from jax import lax
from jax.experimental import pallas as pl
from jax.experimental.pallas import tpu as pltpu
from jax.sharding import PartitionSpec as P

SHARES = (2, 2, 6, 4, 2)
SENDING = (1, 2, 0, 3, 4)
RETURNING = (1, 2, 3, 0, 4)
DISTANCES = (2, 3, 1, 6, 7, 4, 5)

step_length = 0.3
relax_rate = 0.5
coupling = 8.0


F32 = jnp.float32
BF16 = jnp.bfloat16


def ring(count, shift):
    return [(i, (i + shift) % count) for i in range(count)]


def angle_tables(orientations):
    along_x = orientations[0]
    along_y = orientations[1]
    along_z = orientations[2]
    field_terms = jnp.stack(
        [
            along_x * along_x,
            along_y * along_y,
            along_z * along_z,
            2.0 * along_x * along_y,
            2.0 * along_x * along_z,
            2.0 * along_y * along_z,
        ]
    )
    tensor_terms = jnp.stack(
        [
            along_x * along_x - 1.0 / 3.0,
            along_y * along_y - 1.0 / 3.0,
            along_z * along_z - 1.0 / 3.0,
            along_x * along_y,
            along_x * along_z,
            along_y * along_z,
        ]
    )
    return (field_terms, tensor_terms)


def stencil_weights(orientations):
    low = step_length * jnp.maximum(orientations, 0.0)
    high = -step_length * jnp.minimum(orientations, 0.0)
    middle = 1.0 - jnp.sum(low + high, axis=0)
    return jnp.stack([low[0], high[0], low[1], high[1], low[2], high[2], middle])


def paired(owners):
    return owners == len(DISTANCES) + 1


def block_count(owners):
    return owners if paired(owners) else 1


def owner_rows(place, index, rows):
    if place is None:
        return pl.ds(index * rows, rows)
    return pl.ds(pl.multiple_of(jnp.bitwise_xor(place, index) * rows, rows), rows)


def advect_kernel(has_low, has_high, pieces, *refs):
    refs = list(refs)
    coef, place, below, centre, above = refs[:5]
    rest = refs[5:]
    low = rest.pop(0) if has_low else None
    high = rest.pop(0) if has_high else None
    field = rest[0]
    outs = rest[1 : 1 + pieces]
    staged = rest[-1]
    z = pl.program_id(0)
    last = pl.num_programs(0) - 1
    count, width = staged.shape[0], staged.shape[1]
    group, rows = outs[0].shape[0], outs[0].shape[2]

    def one(o, carry):
        f = centre[o, 0].astype(F32)
        zm = below[o, 0].astype(F32)
        if has_low:
            zm = jnp.where(z == 0, low[o, 0].astype(F32), zm)
        zp = above[o, 0].astype(F32)
        if has_high:
            zp = jnp.where(z == last, high[o, 0].astype(F32), zp)
        lanes = f.shape[1]
        moved = coef[6, o] * f
        moved += coef[0, o] * pltpu.roll(f, 1, 1) + coef[1, o] * pltpu.roll(f, lanes - 1, 1)
        moved += coef[2, o] * pltpu.roll(f, 1, 0) + coef[3, o] * pltpu.roll(f, width - 1, 0)
        moved += coef[4, o] * zm + coef[5, o] * zp
        exponent = coef[7, o] * field[0, 0].astype(F32)
        for c in range(1, 6):
            exponent += coef[7 + c, o] * field[c, 0].astype(F32)
        staged[o] = moved * jnp.exp(exponent)
        return carry

    lax.fori_loop(0, count, one, 0)
    base = place[0] if pieces > 1 else None
    for index in range(pieces * group):
        part = staged[:, owner_rows(base, index, rows), :]
        outs[index // group][index % group, 0] = jnp.swapaxes(part, 0, 1).astype(BF16)


def advect(coef, place, q, low, high, field, start, depth, owners):
    count, layers, width, lanes = q.shape
    rows = width // owners
    pieces = block_count(owners)
    group = owners // pieces
    block = (count, 1, width, lanes)
    in_specs = [
        pl.BlockSpec(memory_space=pltpu.SMEM),
        pl.BlockSpec(memory_space=pltpu.SMEM),
        pl.BlockSpec(block, lambda z: (0, jnp.maximum(start + z - 1, 0), 0, 0)),
        pl.BlockSpec(block, lambda z: (0, start + z, 0, 0)),
        pl.BlockSpec(block, lambda z: (0, jnp.minimum(start + z + 1, layers - 1), 0, 0)),
    ]
    operands = [coef, place, q, q, q]
    for halo in (low, high):
        if halo is not None:
            in_specs.append(pl.BlockSpec(block, lambda z: (0, 0, 0, 0)))
            operands.append(halo)
    in_specs.append(pl.BlockSpec((6, 1, width, lanes), lambda z: (0, start + z, 0, 0)))
    operands.append(field)
    cells = count * depth * width * lanes
    return pl.pallas_call(
        functools.partial(advect_kernel, low is not None, high is not None, pieces),
        grid=(depth,),
        in_specs=in_specs,
        out_specs=[pl.BlockSpec((group, 1, rows, count, lanes), lambda z: (0, z, 0, 0, 0))]
        * pieces,
        out_shape=[jax.ShapeDtypeStruct((group, depth, rows, count, lanes), BF16)] * pieces,
        scratch_shapes=[pltpu.VMEM((count, width, lanes), F32)],
        cost_estimate=pl.CostEstimate(
            flops=30 * cells, transcendentals=cells, bytes_accessed=8 * cells
        ),
        name="advect_first",
    )(*operands)


def turn_kernel(pieces, rotation, *refs):
    blocks = refs[:pieces]
    out, south, north = refs[pieces:]
    group, rows, count, lanes = (blocks[0].shape[i] for i in (0, 2, 3, 4))
    pair = 2 if rows % 2 == 0 else 1

    def one(step, carry):
        columns = []
        for j in range(pair):
            y = step * pair + j
            parts = [b[:, 0, y].astype(F32).reshape(group * count, lanes) for b in blocks]
            column = jnp.concatenate(parts, axis=0) if pieces > 1 else parts[0]
            columns.append(column.astype(BF16))
        wide = jnp.concatenate(columns, axis=1) if pair > 1 else columns[0]
        turned = jnp.dot(rotation[...], wide, preferred_element_type=F32).astype(BF16)
        for j in range(pair):
            out[0, step * pair + j] = turned[:, j * lanes : (j + 1) * lanes]
        return carry

    lax.fori_loop(0, rows // pair, one, 0)
    south[0, 0] = out[0, rows - 1]
    north[0, 0] = out[0, 0]


def turn(rotation, blocks):
    pieces = len(blocks)
    group, depth, rows, count, lanes = blocks[0].shape
    total = pieces * group * count
    cells = total * depth * rows * lanes
    edge = pl.BlockSpec((1, 1, total, lanes), lambda z: (z, 0, 0, 0))
    edge_shape = jax.ShapeDtypeStruct((depth, 1, total, lanes), BF16)
    return pl.pallas_call(
        functools.partial(turn_kernel, pieces),
        grid=(depth,),
        in_specs=[pl.BlockSpec((total, total), lambda z: (0, 0))]
        + [pl.BlockSpec((group, 1, rows, count, lanes), lambda z: (0, z, 0, 0, 0))] * pieces,
        out_specs=[pl.BlockSpec((1, rows, total, lanes), lambda z: (z, 0, 0, 0)), edge, edge],
        out_shape=[
            jax.ShapeDtypeStruct((depth, rows, total, lanes), BF16),
            edge_shape,
            edge_shape,
        ],
        cost_estimate=pl.CostEstimate(
            flops=2 * total * cells, transcendentals=0, bytes_accessed=4 * cells
        ),
        name="turn_first",
    )(rotation, *blocks)


def advect_turn_kernel(
    pieces, rotation, weights, terms, below, centre, above, low, high, south, north, field, *refs
):
    outs = refs[:pieces]
    mixed, powers = refs[pieces:]
    z = pl.program_id(0)
    last = pl.num_programs(0) - 1
    rows, total, lanes = centre.shape[1:]
    group, count = outs[0].shape[0], outs[0].shape[3]
    pair = 2 if rows % 2 == 0 else 1
    piece = 64 if total % 64 == 0 else total

    def one(step, carry):
        for j in range(pair):
            y = step * pair + j
            powers[...] = jnp.dot(terms[...], field[0, y], preferred_element_type=F32)
            for base in range(0, total, piece):
                part = pl.ds(base, piece)
                f = centre[0, y, part].astype(F32)
                ym = centre[0, jnp.maximum(y - 1, 0), part].astype(F32)
                ym = jnp.where(y == 0, south[0, 0, part].astype(F32), ym)
                yp = centre[0, jnp.minimum(y + 1, rows - 1), part].astype(F32)
                yp = jnp.where(y == rows - 1, north[0, 0, part].astype(F32), yp)
                zm = below[0, y, part].astype(F32)
                zm = jnp.where(z == 0, low[0, y, part].astype(F32), zm)
                zp = above[0, y, part].astype(F32)
                zp = jnp.where(z == last, high[0, y, part].astype(F32), zp)
                moved = weights[6, part] * f
                moved += weights[0, part] * pltpu.roll(f, 1, 1)
                moved += weights[1, part] * pltpu.roll(f, lanes - 1, 1)
                moved += weights[2, part] * ym + weights[3, part] * yp
                moved += weights[4, part] * zm + weights[5, part] * zp
                mixed[part, j * lanes : (j + 1) * lanes] = (
                    moved * jnp.exp(powers[part])
                ).astype(BF16)
        turned = jnp.dot(rotation[...], mixed[...], preferred_element_type=F32)
        span = group * count
        for j in range(pair):
            column = turned[:, j * lanes : (j + 1) * lanes]
            for p in range(pieces):
                mine = column[p * span : (p + 1) * span]
                outs[p][:, 0, step * pair + j] = mine.reshape(group, count, lanes).astype(BF16)
        return carry

    lax.fori_loop(0, rows // pair, one, 0)


def advect_turn(
    rotation, weights, terms, state, low, high, south, north, field, start, owners
):
    depth, rows, total, lanes = state.shape
    count = total // owners
    pieces = block_count(owners)
    group = owners // pieces
    layer = (1, rows, total, lanes)
    edge = (1, 1, total, lanes)
    pair = 2 if rows % 2 == 0 else 1
    cells = total * depth * rows * lanes
    low_last = low.shape[0] - 1
    here = lambda z: (z, 0, 0, 0)
    return pl.pallas_call(
        functools.partial(advect_turn_kernel, pieces),
        grid=(depth,),
        in_specs=[
            pl.BlockSpec((total, total), lambda z: (0, 0)),
            pl.BlockSpec(weights.shape, lambda z: (0, 0, 0)),
            pl.BlockSpec(terms.shape, lambda z: (0, 0)),
            pl.BlockSpec(layer, lambda z: (jnp.maximum(z - 1, 0), 0, 0, 0)),
            pl.BlockSpec(layer, here),
            pl.BlockSpec(layer, lambda z: (jnp.minimum(z + 1, depth - 1), 0, 0, 0)),
            pl.BlockSpec(layer, lambda z: (low_last, 0, 0, 0)),
            pl.BlockSpec(layer, lambda z: (0, 0, 0, 0)),
            pl.BlockSpec(edge, here),
            pl.BlockSpec(edge, here),
            pl.BlockSpec((1,) + field.shape[1:], lambda z: (start + z, 0, 0, 0)),
        ],
        out_specs=[pl.BlockSpec((group, 1, rows, count, lanes), lambda z: (0, z, 0, 0, 0))]
        * pieces,
        out_shape=[jax.ShapeDtypeStruct((group, depth, rows, count, lanes), BF16)] * pieces,
        scratch_shapes=[
            pltpu.VMEM((total, pair * lanes), BF16),
            pltpu.VMEM((total, lanes), F32),
        ],
        cost_estimate=pl.CostEstimate(
            flops=2 * total * cells, transcendentals=cells, bytes_accessed=8 * cells
        ),
        name="advect_turn",
    )(rotation, weights, terms, state, state, state, low, high, south, north, field)


def gather_kernel(pieces, by_owner, coef, place, *refs):
    blocks = refs[:pieces]
    partner = refs[pieces]
    state, partial = refs[-2:]
    group, rows, count = (blocks[0].shape[i] for i in (0, 2, 3))
    base = place[0] if pieces > 1 else None
    for index in range(pieces * group):
        part = owner_rows(base, index, rows)
        slot = jnp.bitwise_xor(base, index) if by_owner and pieces > 1 else index
        block = blocks[index // group]
        mine = jnp.swapaxes(block[index % group, 0].astype(F32), 0, 1)
        state[:, 0, part, :] = mine.astype(BF16)
        sums = [None] * 6
        for o in range(count):
            product = mine[o] * partner[o, 0, part, :].astype(F32)
            for c in range(6):
                term = coef[c, o] * product
                sums[c] = term if sums[c] is None else sums[c] + term
        for c in range(6):
            partial[slot, c, 0] = sums[c].astype(partial.dtype)


def gather(coef, place, blocks, partner, state, start, closing):
    pieces = len(blocks)
    group, depth, rows, count, lanes = blocks[0].shape
    owners = pieces * group
    width = partner.shape[2]
    cells = owners * depth * rows * count * lanes
    slab = pl.BlockSpec((count, 1, width, lanes), lambda z: (0, start + z, 0, 0))
    operands = [coef, place, *blocks, partner]
    in_specs = (
        [pl.BlockSpec(memory_space=pltpu.SMEM)] * 2
        + [pl.BlockSpec((group, 1, rows, count, lanes), lambda z: (0, z, 0, 0, 0))] * pieces
        + [slab]
    )
    aliases = {}
    if state is not None:
        aliases = {len(operands): 0}
        operands.append(state)
        in_specs.append(pl.BlockSpec(memory_space=pl.ANY))
    return pl.pallas_call(
        functools.partial(gather_kernel, pieces, closing),
        grid=(depth,),
        in_specs=in_specs,
        out_specs=[
            slab,
            pl.BlockSpec((owners, 6, 1, rows, lanes), lambda z: (0, 0, z, 0, 0)),
        ],
        out_shape=[
            jax.ShapeDtypeStruct(partner.shape, BF16),
            jax.ShapeDtypeStruct(
                (owners, 6, depth, rows, lanes), BF16 if closing else F32
            ),
        ],
        input_output_aliases=aliases,
        cost_estimate=pl.CostEstimate(
            flops=14 * cells, transcendentals=0, bytes_accessed=6 * cells
        ),
        name="gather_last",
    )(*operands)


def swapped(block, distance):
    owners = lax.axis_size("orient")
    return lax.ppermute(block, "orient", [(i, i ^ distance) for i in range(owners)])


def exchange(block):
    return lax.all_to_all(block, "orient", split_axis=0, concat_axis=0, tiled=True)


def exchange_blocks(blocks):
    if len(blocks) == 1:
        return [exchange(blocks[0])]
    came = list(blocks)
    for distance in DISTANCES:
        came[distance] = swapped(blocks[distance], distance)
    return came


def halve(held):
    stride = 1
    while held.shape[0] > 1:
        half = held.shape[0] // 2
        pairs = held.reshape((half, 2) + held.shape[1:])
        theirs = pairs[:, 1]
        if half == 1:
            theirs = theirs.astype(BF16)
        came = swapped(theirs, stride)
        held = pairs[:, 0] + came.astype(F32)
        stride *= 2
    return held[0]


def chunk_sizes(layers):
    whole = sum(SHARES)
    sizes = [max(1, layers * share // whole) for share in SHARES]
    sizes[2] += layers - sum(sizes)
    return sizes


def staged_device(q_init, partner, field, orientations, orient_weight, rotation):
    owners = lax.axis_size("orient")
    slabs = lax.axis_size("space")
    me = lax.axis_index("orient")
    count, layers, width, lanes = q_init.shape
    total = rotation.shape[0]
    rows = width // owners
    sizes = chunk_sizes(layers)
    chunks = len(sizes)
    starts = [sum(sizes[:c]) for c in range(chunks)]
    place = me.astype(jnp.int32).reshape(1)

    first = lax.ppermute(q_init[:, layers - 1 :], "space", ring(slabs, 1))
    final = lax.ppermute(q_init[:, :1], "space", ring(slabs, -1))

    field_terms, tensor_terms = angle_tables(orientations)
    weights = stencil_weights(orientations)
    exponent_terms = -step_length * field_terms
    local_coef = lax.dynamic_slice_in_dim(
        jnp.concatenate([weights, exponent_terms]), me * count, count, 1
    )
    local_tensor = lax.dynamic_slice_in_dim(
        tensor_terms * orient_weight[None, :], me * count, count, 1
    )
    wide_weights = jnp.broadcast_to(weights[:, :, None], weights.shape + (lanes,))
    top = lax.reduce_precision(exponent_terms, 8, 7)
    left = exponent_terms - top
    centre = lax.reduce_precision(left, 8, 7)
    split_terms = jnp.concatenate([top, centre, left - centre]).astype(BF16).T
    own_field = lax.dynamic_slice_in_dim(field, me * rows, rows, 2)
    row_field = jnp.transpose(own_field, (1, 2, 0, 3))
    row_field = jnp.concatenate([row_field] * 3, axis=2)
    padding = 32 - split_terms.shape[1]
    split_terms = jnp.pad(split_terms, ((0, 0), (0, padding)))
    row_field = jnp.pad(row_field, ((0, 0), (0, 0), (0, padding), (0, 0)))
    enter = rotation
    leave = rotation
    if paired(owners):
        into = lax.broadcasted_iota(jnp.int32, (total, total), 1)
        source = ((into // count) ^ me) * count + into % count
        chosen = (lax.broadcasted_iota(jnp.int32, (total, total), 0) == source).astype(BF16)
        enter = jnp.dot(rotation, chosen, preferred_element_type=F32).astype(BF16)
        leave = jnp.dot(chosen.T, rotation, preferred_element_type=F32).astype(BF16)

    turned = {}
    souths = {}
    norths = {}
    for c in SENDING:
        sent = advect(
            local_coef,
            place,
            q_init,
            first if c == 0 else None,
            final if c == chunks - 1 else None,
            field,
            starts[c],
            sizes[c],
            owners,
        )
        got = exchange_blocks(sent)
        turned[c], top_rows, end_rows = turn(enter, got)
        souths[c] = lax.ppermute(top_rows, "orient", ring(owners, 1))
        norths[c] = lax.ppermute(end_rows, "orient", ring(owners, -1))
    under = lax.ppermute(turned[chunks - 1][-1:], "space", ring(slabs, 1))
    over = lax.ppermute(turned[0][:1], "space", ring(slabs, -1))

    state = None
    sums = {}
    for c in RETURNING:
        sent = advect_turn(
            leave,
            wide_weights,
            split_terms,
            turned[c],
            under if c == 0 else turned[c - 1],
            over if c == chunks - 1 else turned[c + 1],
            souths[c],
            norths[c],
            row_field,
            starts[c],
            owners,
        )
        got = exchange_blocks(sent)
        closing = c == RETURNING[-1] or not paired(owners)
        state, partial = gather(
            local_tensor, place, got, partner, state, starts[c], closing
        )
        if closing:
            sums[c] = jnp.sum(exchange(partial).astype(F32), axis=0)
        else:
            sums[c] = halve(partial)
    tensor = jnp.concatenate([sums[c] for c in range(chunks)], axis=1)
    new_field = (1.0 - relax_rate) * own_field.astype(F32) + relax_rate * coupling * tensor
    return (state, new_field)


def solution(mesh):
    in_specs = (
        P("orient", "space", None, None),
        P("orient", "space", None, None),
        P(None, "space", None, None),
        P(),
        P(),
        P(),
    )
    out_specs = (P("orient", "space", None, None), P(None, "space", "orient", None))
    mapped = jax.shard_map(
        staged_device, mesh=mesh, in_specs=in_specs, out_specs=out_specs, check_vma=False
    )
    if not paired(mesh.shape["orient"]):
        return mapped
    return mapped
```

```python
import functools

import jax
import jax.numpy as jnp
from jax import lax
from jax.experimental import pallas as pl
from jax.experimental.pallas import tpu as pltpu
from jax.sharding import PartitionSpec as P

SHARES = (2, 3, 5, 5, 1)
SENDING = (1, 2, 0, 3, 4)
RETURNING = (1, 2, 3, 0, 4)
CLOSING = RETURNING[-2:]
DISTANCES = (2, 3, 1, 6, 7, 4, 5)

step_length = 0.3
relax_rate = 0.5
coupling = 8.0


F32 = jnp.float32
BF16 = jnp.bfloat16


def ring(count, shift):
    return [(i, (i + shift) % count) for i in range(count)]


def angle_tables(orientations):
    along_x = orientations[0]
    along_y = orientations[1]
    along_z = orientations[2]
    field_terms = jnp.stack(
        [
            along_x * along_x,
            along_y * along_y,
            along_z * along_z,
            2.0 * along_x * along_y,
            2.0 * along_x * along_z,
            2.0 * along_y * along_z,
        ]
    )
    tensor_terms = jnp.stack(
        [
            along_x * along_x - 1.0 / 3.0,
            along_y * along_y - 1.0 / 3.0,
            along_z * along_z - 1.0 / 3.0,
            along_x * along_y,
            along_x * along_z,
            along_y * along_z,
        ]
    )
    return (field_terms, tensor_terms)


def stencil_weights(orientations):
    low = step_length * jnp.maximum(orientations, 0.0)
    high = -step_length * jnp.minimum(orientations, 0.0)
    middle = 1.0 - jnp.sum(low + high, axis=0)
    return jnp.stack([low[0], high[0], low[1], high[1], low[2], high[2], middle])


def paired(owners):
    return owners == len(DISTANCES) + 1


def block_count(owners):
    return owners if paired(owners) else 1


def owner_rows(place, index, rows):
    if place is None:
        return pl.ds(index * rows, rows)
    return pl.ds(pl.multiple_of(jnp.bitwise_xor(place, index) * rows, rows), rows)


def advect_kernel(has_low, has_high, pieces, *refs):
    refs = list(refs)
    coef, place, below, centre, above = refs[:5]
    rest = refs[5:]
    low = rest.pop(0) if has_low else None
    high = rest.pop(0) if has_high else None
    field = rest[0]
    outs = rest[1 : 1 + pieces]
    staged = rest[-1]
    z = pl.program_id(0)
    last = pl.num_programs(0) - 1
    count, width = staged.shape[0], staged.shape[1]
    group, rows = outs[0].shape[0], outs[0].shape[2]

    first = place[0] * count

    def one(o, carry):
        f = centre[o, 0].astype(F32)
        zm = below[o, 0].astype(F32)
        if has_low:
            zm = jnp.where(z == 0, low[o, 0].astype(F32), zm)
        zp = above[o, 0].astype(F32)
        if has_high:
            zp = jnp.where(z == last, high[o, 0].astype(F32), zp)
        lanes = f.shape[1]
        ux, uy, uz = (coef[axis, first + o] for axis in range(3))
        moved = (1.0 - step_length * (jnp.abs(ux) + jnp.abs(uy) + jnp.abs(uz))) * f
        sides = (
            (pltpu.roll(f, 1, 1), pltpu.roll(f, lanes - 1, 1)),
            (pltpu.roll(f, 1, 0), pltpu.roll(f, width - 1, 0)),
            (zm, zp),
        )
        for u, (back, fore) in zip((ux, uy, uz), sides):
            moved += (step_length * jnp.maximum(u, 0.0)) * back
            moved -= (step_length * jnp.minimum(u, 0.0)) * fore
        terms = (ux * ux, uy * uy, uz * uz, 2.0 * ux * uy, 2.0 * ux * uz, 2.0 * uy * uz)
        exponent = (-step_length * terms[0]) * field[0, 0].astype(F32)
        for c in range(1, 6):
            exponent += (-step_length * terms[c]) * field[c, 0].astype(F32)
        staged[o] = moved * jnp.exp(exponent)
        return carry

    lax.fori_loop(0, count, one, 0)
    base = place[0] if pieces > 1 else None
    for index in range(pieces * group):
        part = staged[:, owner_rows(base, index, rows), :]
        outs[index // group][index % group, 0] = jnp.swapaxes(part, 0, 1).astype(BF16)


def advect(coef, place, q, low, high, field, start, depth, owners):
    count, layers, width, lanes = q.shape
    rows = width // owners
    pieces = block_count(owners)
    group = owners // pieces
    block = (count, 1, width, lanes)
    in_specs = [
        pl.BlockSpec(memory_space=pltpu.SMEM),
        pl.BlockSpec(memory_space=pltpu.SMEM),
        pl.BlockSpec(block, lambda z: (0, jnp.maximum(start + z - 1, 0), 0, 0)),
        pl.BlockSpec(block, lambda z: (0, start + z, 0, 0)),
        pl.BlockSpec(block, lambda z: (0, jnp.minimum(start + z + 1, layers - 1), 0, 0)),
    ]
    operands = [coef, place, q, q, q]
    for halo in (low, high):
        if halo is not None:
            in_specs.append(pl.BlockSpec(block, lambda z: (0, 0, 0, 0)))
            operands.append(halo)
    in_specs.append(pl.BlockSpec((6, 1, width, lanes), lambda z: (0, start + z, 0, 0)))
    operands.append(field)
    cells = count * depth * width * lanes
    return pl.pallas_call(
        functools.partial(advect_kernel, low is not None, high is not None, pieces),
        grid=(depth,),
        in_specs=in_specs,
        out_specs=[pl.BlockSpec((group, 1, rows, count, lanes), lambda z: (0, z, 0, 0, 0))]
        * pieces,
        out_shape=[jax.ShapeDtypeStruct((group, depth, rows, count, lanes), BF16)] * pieces,
        scratch_shapes=[pltpu.VMEM((count, width, lanes), F32)],
        cost_estimate=pl.CostEstimate(
            flops=30 * cells, transcendentals=cells, bytes_accessed=8 * cells
        ),
        name="advect_first",
    )(*operands)


def turn_kernel(pieces, rotation, *refs):
    blocks = refs[:pieces]
    out, south, north = refs[pieces:]
    group, rows, count, lanes = (blocks[0].shape[i] for i in (0, 2, 3, 4))
    pair = 2 if rows % 2 == 0 else 1

    def one(step, carry):
        columns = []
        for j in range(pair):
            y = step * pair + j
            parts = [b[:, 0, y].astype(F32).reshape(group * count, lanes) for b in blocks]
            column = jnp.concatenate(parts, axis=0) if pieces > 1 else parts[0]
            columns.append(column.astype(BF16))
        wide = jnp.concatenate(columns, axis=1) if pair > 1 else columns[0]
        turned = jnp.dot(rotation[...], wide, preferred_element_type=F32).astype(BF16)
        for j in range(pair):
            out[0, step * pair + j] = turned[:, j * lanes : (j + 1) * lanes]
        return carry

    lax.fori_loop(0, rows // pair, one, 0)
    south[0, 0] = out[0, rows - 1]
    north[0, 0] = out[0, 0]


def turn(rotation, blocks):
    pieces = len(blocks)
    group, depth, rows, count, lanes = blocks[0].shape
    total = pieces * group * count
    cells = total * depth * rows * lanes
    edge = pl.BlockSpec((1, 1, total, lanes), lambda z: (z, 0, 0, 0))
    edge_shape = jax.ShapeDtypeStruct((depth, 1, total, lanes), BF16)
    return pl.pallas_call(
        functools.partial(turn_kernel, pieces),
        grid=(depth,),
        in_specs=[pl.BlockSpec((total, total), lambda z: (0, 0))]
        + [pl.BlockSpec((group, 1, rows, count, lanes), lambda z: (0, z, 0, 0, 0))] * pieces,
        out_specs=[pl.BlockSpec((1, rows, total, lanes), lambda z: (z, 0, 0, 0)), edge, edge],
        out_shape=[
            jax.ShapeDtypeStruct((depth, rows, total, lanes), BF16),
            edge_shape,
            edge_shape,
        ],
        cost_estimate=pl.CostEstimate(
            flops=2 * total * cells, transcendentals=0, bytes_accessed=4 * cells
        ),
        name="turn_first",
    )(rotation, *blocks)


def advect_turn_kernel(
    pieces, rotation, weights, terms, below, centre, above, low, high, south, north, field, *refs
):
    outs = refs[:pieces]
    mixed, powers = refs[pieces:]
    z = pl.program_id(0)
    last = pl.num_programs(0) - 1
    rows, total, lanes = centre.shape[1:]
    group, count = outs[0].shape[0], outs[0].shape[3]
    pair = 2 if rows % 2 == 0 else 1
    piece = 64 if total % 64 == 0 else total

    def one(step, carry):
        for j in range(pair):
            y = step * pair + j
            powers[...] = jnp.dot(terms[...], field[0, y], preferred_element_type=F32)
            for base in range(0, total, piece):
                part = pl.ds(base, piece)
                f = centre[0, y, part].astype(F32)
                ym = centre[0, jnp.maximum(y - 1, 0), part].astype(F32)
                ym = jnp.where(y == 0, south[0, 0, part].astype(F32), ym)
                yp = centre[0, jnp.minimum(y + 1, rows - 1), part].astype(F32)
                yp = jnp.where(y == rows - 1, north[0, 0, part].astype(F32), yp)
                zm = below[0, y, part].astype(F32)
                zm = jnp.where(z == 0, low[0, y, part].astype(F32), zm)
                zp = above[0, y, part].astype(F32)
                zp = jnp.where(z == last, high[0, y, part].astype(F32), zp)
                moved = weights[6, part] * f
                moved += weights[0, part] * pltpu.roll(f, 1, 1)
                moved += weights[1, part] * pltpu.roll(f, lanes - 1, 1)
                moved += weights[2, part] * ym + weights[3, part] * yp
                moved += weights[4, part] * zm + weights[5, part] * zp
                mixed[part, j * lanes : (j + 1) * lanes] = (
                    moved * jnp.exp(powers[part])
                ).astype(BF16)
        turned = jnp.dot(rotation[...], mixed[...], preferred_element_type=F32)
        span = group * count
        for j in range(pair):
            column = turned[:, j * lanes : (j + 1) * lanes]
            for p in range(pieces):
                mine = column[p * span : (p + 1) * span]
                outs[p][:, 0, step * pair + j] = mine.reshape(group, count, lanes).astype(BF16)
        return carry

    lax.fori_loop(0, rows // pair, one, 0)


def advect_turn(
    rotation, weights, terms, state, low, high, south, north, field, start, owners
):
    depth, rows, total, lanes = state.shape
    count = total // owners
    pieces = block_count(owners)
    group = owners // pieces
    layer = (1, rows, total, lanes)
    edge = (1, 1, total, lanes)
    pair = 2 if rows % 2 == 0 else 1
    cells = total * depth * rows * lanes
    low_last = low.shape[0] - 1
    here = lambda z: (z, 0, 0, 0)
    return pl.pallas_call(
        functools.partial(advect_turn_kernel, pieces),
        grid=(depth,),
        in_specs=[
            pl.BlockSpec((total, total), lambda z: (0, 0)),
            pl.BlockSpec(weights.shape, lambda z: (0, 0, 0)),
            pl.BlockSpec(terms.shape, lambda z: (0, 0)),
            pl.BlockSpec(layer, lambda z: (jnp.maximum(z - 1, 0), 0, 0, 0)),
            pl.BlockSpec(layer, here),
            pl.BlockSpec(layer, lambda z: (jnp.minimum(z + 1, depth - 1), 0, 0, 0)),
            pl.BlockSpec(layer, lambda z: (low_last, 0, 0, 0)),
            pl.BlockSpec(layer, lambda z: (0, 0, 0, 0)),
            pl.BlockSpec(edge, here),
            pl.BlockSpec(edge, here),
            pl.BlockSpec((1,) + field.shape[1:], lambda z: (start + z, 0, 0, 0)),
        ],
        out_specs=[pl.BlockSpec((group, 1, rows, count, lanes), lambda z: (0, z, 0, 0, 0))]
        * pieces,
        out_shape=[jax.ShapeDtypeStruct((group, depth, rows, count, lanes), BF16)] * pieces,
        scratch_shapes=[
            pltpu.VMEM((total, pair * lanes), BF16),
            pltpu.VMEM((total, lanes), F32),
        ],
        cost_estimate=pl.CostEstimate(
            flops=2 * total * cells, transcendentals=cells, bytes_accessed=8 * cells
        ),
        name="advect_turn",
    )(rotation, weights, terms, state, state, state, low, high, south, north, field)


def gather_kernel(pieces, by_owner, coef, place, *refs):
    blocks = refs[:pieces]
    partner = refs[pieces]
    state, partial = refs[-2:]
    group, rows, count = (blocks[0].shape[i] for i in (0, 2, 3))
    base = place[0] if pieces > 1 else None
    for index in range(pieces * group):
        part = owner_rows(base, index, rows)
        slot = jnp.bitwise_xor(base, index) if by_owner and pieces > 1 else index
        block = blocks[index // group]
        mine = jnp.swapaxes(block[index % group, 0].astype(F32), 0, 1)
        state[:, 0, part, :] = mine.astype(BF16)
        sums = [None] * 6
        for o in range(count):
            product = mine[o] * partner[o, 0, part, :].astype(F32)
            for c in range(6):
                term = coef[c, o] * product
                sums[c] = term if sums[c] is None else sums[c] + term
        for c in range(6):
            partial[slot, c, 0] = sums[c].astype(partial.dtype)


def gather(coef, place, blocks, partner, state, start, closing):
    pieces = len(blocks)
    group, depth, rows, count, lanes = blocks[0].shape
    owners = pieces * group
    width = partner.shape[2]
    cells = owners * depth * rows * count * lanes
    slab = pl.BlockSpec((count, 1, width, lanes), lambda z: (0, start + z, 0, 0))
    operands = [coef, place, *blocks, partner]
    in_specs = (
        [pl.BlockSpec(memory_space=pltpu.SMEM)] * 2
        + [pl.BlockSpec((group, 1, rows, count, lanes), lambda z: (0, z, 0, 0, 0))] * pieces
        + [slab]
    )
    aliases = {}
    if state is not None:
        aliases = {len(operands): 0}
        operands.append(state)
        in_specs.append(pl.BlockSpec(memory_space=pl.ANY))
    return pl.pallas_call(
        functools.partial(gather_kernel, pieces, closing),
        grid=(depth,),
        in_specs=in_specs,
        out_specs=[
            slab,
            pl.BlockSpec((owners, 6, 1, rows, lanes), lambda z: (0, 0, z, 0, 0)),
        ],
        out_shape=[
            jax.ShapeDtypeStruct(partner.shape, BF16),
            jax.ShapeDtypeStruct(
                (owners, 6, depth, rows, lanes), BF16 if closing else F32
            ),
        ],
        input_output_aliases=aliases,
        cost_estimate=pl.CostEstimate(
            flops=14 * cells, transcendentals=0, bytes_accessed=6 * cells
        ),
        name="gather_last",
    )(*operands)


def swapped(block, distance):
    owners = lax.axis_size("orient")
    return lax.ppermute(block, "orient", [(i, i ^ distance) for i in range(owners)])


def exchange(block):
    return lax.all_to_all(block, "orient", split_axis=0, concat_axis=0, tiled=True)


def exchange_blocks(blocks):
    if len(blocks) == 1:
        return [exchange(blocks[0])]
    came = list(blocks)
    for distance in DISTANCES:
        came[distance] = swapped(blocks[distance], distance)
    return came


def halve(held, narrow):
    stride = 1
    while held.shape[0] > 1:
        half = held.shape[0] // 2
        pairs = held.reshape((half, 2) + held.shape[1:])
        theirs = pairs[:, 1]
        if narrow or half == 1:
            theirs = theirs.astype(BF16)
        came = swapped(theirs, stride)
        held = pairs[:, 0] + came.astype(F32)
        stride *= 2
    return held[0]


def chunk_sizes(layers):
    whole = sum(SHARES)
    sizes = [max(1, layers * share // whole) for share in SHARES]
    sizes[2] += layers - sum(sizes)
    return sizes


def staged_device(q_init, partner, field, orientations, orient_weight, rotation):
    owners = lax.axis_size("orient")
    slabs = lax.axis_size("space")
    me = lax.axis_index("orient")
    count, layers, width, lanes = q_init.shape
    total = rotation.shape[0]
    rows = width // owners
    sizes = chunk_sizes(layers)
    chunks = len(sizes)
    starts = [sum(sizes[:c]) for c in range(chunks)]
    place = me.astype(jnp.int32).reshape(1)

    first = lax.ppermute(q_init[:, layers - 1 :], "space", ring(slabs, 1))
    final = lax.ppermute(q_init[:, :1], "space", ring(slabs, -1))

    field_terms, tensor_terms = angle_tables(orientations)
    weights = stencil_weights(orientations)
    exponent_terms = -step_length * field_terms
    local_tensor = lax.dynamic_slice_in_dim(
        tensor_terms * orient_weight[None, :], me * count, count, 1
    )
    wide_weights = jnp.broadcast_to(weights[:, :, None], weights.shape + (lanes,))
    top = lax.reduce_precision(exponent_terms, 8, 7)
    left = exponent_terms - top
    centre = lax.reduce_precision(left, 8, 7)
    split_terms = jnp.concatenate([top, centre, left - centre]).astype(BF16).T
    own_field = lax.dynamic_slice_in_dim(field, me * rows, rows, 2)
    row_field = jnp.transpose(own_field, (1, 2, 0, 3))
    row_field = jnp.concatenate([row_field] * 3, axis=2)
    padding = 32 - split_terms.shape[1]
    split_terms = jnp.pad(split_terms, ((0, 0), (0, padding)))
    row_field = jnp.pad(row_field, ((0, 0), (0, 0), (0, padding), (0, 0)))
    enter = rotation
    leave = rotation
    if paired(owners):
        into = lax.broadcasted_iota(jnp.int32, (total, total), 1)
        source = ((into // count) ^ me) * count + into % count
        chosen = (lax.broadcasted_iota(jnp.int32, (total, total), 0) == source).astype(BF16)
        enter = jnp.dot(rotation, chosen, preferred_element_type=F32).astype(BF16)
        leave = jnp.dot(chosen.T, rotation, preferred_element_type=F32).astype(BF16)

    turned = {}
    souths = {}
    norths = {}
    for c in SENDING:
        sent = advect(
            orientations,
            place,
            q_init,
            first if c == 0 else None,
            final if c == chunks - 1 else None,
            field,
            starts[c],
            sizes[c],
            owners,
        )
        got = exchange_blocks(sent)
        turned[c], top_rows, end_rows = turn(enter, got)
        souths[c] = lax.ppermute(top_rows, "orient", ring(owners, 1))
        norths[c] = lax.ppermute(end_rows, "orient", ring(owners, -1))
    under = lax.ppermute(turned[chunks - 1][-1:], "space", ring(slabs, 1))
    over = lax.ppermute(turned[0][:1], "space", ring(slabs, -1))

    state = None
    sums = {}
    for c in RETURNING:
        sent = advect_turn(
            leave,
            wide_weights,
            split_terms,
            turned[c],
            under if c == 0 else turned[c - 1],
            over if c == chunks - 1 else turned[c + 1],
            souths[c],
            norths[c],
            row_field,
            starts[c],
            owners,
        )
        got = exchange_blocks(sent)
        closing = c in CLOSING or not paired(owners)
        state, partial = gather(
            local_tensor, place, got, partner, state, starts[c], closing
        )
        if closing:
            sums[c] = jnp.sum(exchange(partial).astype(F32), axis=0)
        else:
            sums[c] = halve(partial, c == RETURNING[2])
    tensor = jnp.concatenate([sums[c] for c in range(chunks)], axis=1)
    new_field = (1.0 - relax_rate) * own_field.astype(F32) + relax_rate * coupling * tensor
    return (state, new_field)


def solution(mesh):
    in_specs = (
        P("orient", "space", None, None),
        P("orient", "space", None, None),
        P(None, "space", None, None),
        P(),
        P(),
        P(),
    )
    out_specs = (P("orient", "space", None, None), P(None, "space", "orient", None))
    mapped = jax.shard_map(
        staged_device, mesh=mesh, in_specs=in_specs, out_specs=out_specs, check_vma=False
    )
    if not paired(mesh.shape["orient"]):
        return mapped
    return mapped
```

```python
import functools

import jax
import jax.numpy as jnp
from jax import lax
from jax.experimental import pallas as pl
from jax.experimental.pallas import tpu as pltpu
from jax.sharding import PartitionSpec as P

SHARES = (2, 3, 5, 5, 1)
SENDING = (1, 2, 0, 3, 4)
RETURNING = (1, 2, 3, 0, 4)
CLOSING = RETURNING[-2:]
DISTANCES = (2, 3, 1, 6, 7, 4, 5)

step_length = 0.3
relax_rate = 0.5
coupling = 8.0


F32 = jnp.float32
BF16 = jnp.bfloat16


def ring(count, shift):
    return [(i, (i + shift) % count) for i in range(count)]


def angle_tables(orientations):
    along_x = orientations[0]
    along_y = orientations[1]
    along_z = orientations[2]
    field_terms = jnp.stack(
        [
            along_x * along_x,
            along_y * along_y,
            along_z * along_z,
            2.0 * along_x * along_y,
            2.0 * along_x * along_z,
            2.0 * along_y * along_z,
        ]
    )
    tensor_terms = jnp.stack(
        [
            along_x * along_x - 1.0 / 3.0,
            along_y * along_y - 1.0 / 3.0,
            along_z * along_z - 1.0 / 3.0,
            along_x * along_y,
            along_x * along_z,
            along_y * along_z,
        ]
    )
    return (field_terms, tensor_terms)


def stencil_weights(orientations):
    low = step_length * jnp.maximum(orientations, 0.0)
    high = -step_length * jnp.minimum(orientations, 0.0)
    middle = 1.0 - jnp.sum(low + high, axis=0)
    return jnp.stack([low[0], high[0], low[1], high[1], low[2], high[2], middle])


def paired(owners):
    return owners == len(DISTANCES) + 1


def block_count(owners):
    return owners if paired(owners) else 1


def owner_rows(place, index, rows):
    if place is None:
        return pl.ds(index * rows, rows)
    return pl.ds(pl.multiple_of(jnp.bitwise_xor(place, index) * rows, rows), rows)


def advect_kernel(has_low, has_high, pieces, *refs):
    refs = list(refs)
    coef, place, below, centre, above = refs[:5]
    rest = refs[5:]
    low = rest.pop(0) if has_low else None
    high = rest.pop(0) if has_high else None
    field = rest[0]
    outs = rest[1 : 1 + pieces]
    staged = rest[-1]
    z = pl.program_id(0)
    last = pl.num_programs(0) - 1
    count, width = staged.shape[0], staged.shape[1]
    group, rows = outs[0].shape[0], outs[0].shape[2]

    first = place[0] * count

    def one(o, carry):
        f = centre[o, 0].astype(F32)
        zm = below[o, 0].astype(F32)
        if has_low:
            zm = jnp.where(z == 0, low[o, 0].astype(F32), zm)
        zp = above[o, 0].astype(F32)
        if has_high:
            zp = jnp.where(z == last, high[o, 0].astype(F32), zp)
        lanes = f.shape[1]
        ux, uy, uz = (coef[axis, first + o] for axis in range(3))
        moved = (1.0 - step_length * (jnp.abs(ux) + jnp.abs(uy) + jnp.abs(uz))) * f
        sides = (
            (pltpu.roll(f, 1, 1), pltpu.roll(f, lanes - 1, 1)),
            (pltpu.roll(f, 1, 0), pltpu.roll(f, width - 1, 0)),
            (zm, zp),
        )
        for u, (back, fore) in zip((ux, uy, uz), sides):
            moved += (step_length * jnp.maximum(u, 0.0)) * back
            moved -= (step_length * jnp.minimum(u, 0.0)) * fore
        terms = (ux * ux, uy * uy, uz * uz, 2.0 * ux * uy, 2.0 * ux * uz, 2.0 * uy * uz)
        exponent = (-step_length * terms[0]) * field[0, 0].astype(F32)
        for c in range(1, 6):
            exponent += (-step_length * terms[c]) * field[c, 0].astype(F32)
        staged[o] = moved * jnp.exp(exponent)
        return carry

    lax.fori_loop(0, count, one, 0)
    base = place[0] if pieces > 1 else None
    for index in range(pieces * group):
        part = staged[:, owner_rows(base, index, rows), :]
        outs[index // group][index % group, 0] = jnp.swapaxes(part, 0, 1).astype(BF16)


def advect(coef, place, q, low, high, field, start, depth, owners):
    count, layers, width, lanes = q.shape
    rows = width // owners
    pieces = block_count(owners)
    group = owners // pieces
    block = (count, 1, width, lanes)
    in_specs = [
        pl.BlockSpec(memory_space=pltpu.SMEM),
        pl.BlockSpec(memory_space=pltpu.SMEM),
        pl.BlockSpec(block, lambda z: (0, jnp.maximum(start + z - 1, 0), 0, 0)),
        pl.BlockSpec(block, lambda z: (0, start + z, 0, 0)),
        pl.BlockSpec(block, lambda z: (0, jnp.minimum(start + z + 1, layers - 1), 0, 0)),
    ]
    operands = [coef, place, q, q, q]
    for halo in (low, high):
        if halo is not None:
            in_specs.append(pl.BlockSpec(block, lambda z: (0, 0, 0, 0)))
            operands.append(halo)
    in_specs.append(pl.BlockSpec((6, 1, width, lanes), lambda z: (0, start + z, 0, 0)))
    operands.append(field)
    cells = count * depth * width * lanes
    return pl.pallas_call(
        functools.partial(advect_kernel, low is not None, high is not None, pieces),
        grid=(depth,),
        in_specs=in_specs,
        out_specs=[pl.BlockSpec((group, 1, rows, count, lanes), lambda z: (0, z, 0, 0, 0))]
        * pieces,
        out_shape=[jax.ShapeDtypeStruct((group, depth, rows, count, lanes), BF16)] * pieces,
        scratch_shapes=[pltpu.VMEM((count, width, lanes), F32)],
        cost_estimate=pl.CostEstimate(
            flops=30 * cells, transcendentals=cells, bytes_accessed=8 * cells
        ),
        name="advect_first",
    )(*operands)


def turn_kernel(pieces, rotation, *refs):
    blocks = refs[:pieces]
    out, south, north = refs[pieces:]
    group, rows, count, lanes = (blocks[0].shape[i] for i in (0, 2, 3, 4))
    pair = 2 if rows % 2 == 0 else 1

    def one(step, carry):
        columns = []
        for j in range(pair):
            y = step * pair + j
            parts = [b[:, 0, y].astype(F32).reshape(group * count, lanes) for b in blocks]
            column = jnp.concatenate(parts, axis=0) if pieces > 1 else parts[0]
            columns.append(column.astype(BF16))
        wide = jnp.concatenate(columns, axis=1) if pair > 1 else columns[0]
        turned = jnp.dot(rotation[...], wide, preferred_element_type=F32).astype(BF16)
        for j in range(pair):
            out[0, step * pair + j] = turned[:, j * lanes : (j + 1) * lanes]
        return carry

    lax.fori_loop(0, rows // pair, one, 0)
    south[0, 0] = out[0, rows - 1]
    north[0, 0] = out[0, 0]


def turn(rotation, blocks):
    pieces = len(blocks)
    group, depth, rows, count, lanes = blocks[0].shape
    total = pieces * group * count
    cells = total * depth * rows * lanes
    edge = pl.BlockSpec((1, 1, total, lanes), lambda z: (z, 0, 0, 0))
    edge_shape = jax.ShapeDtypeStruct((depth, 1, total, lanes), BF16)
    return pl.pallas_call(
        functools.partial(turn_kernel, pieces),
        grid=(depth,),
        in_specs=[pl.BlockSpec((total, total), lambda z: (0, 0))]
        + [pl.BlockSpec((group, 1, rows, count, lanes), lambda z: (0, z, 0, 0, 0))] * pieces,
        out_specs=[pl.BlockSpec((1, rows, total, lanes), lambda z: (z, 0, 0, 0)), edge, edge],
        out_shape=[
            jax.ShapeDtypeStruct((depth, rows, total, lanes), BF16),
            edge_shape,
            edge_shape,
        ],
        cost_estimate=pl.CostEstimate(
            flops=2 * total * cells, transcendentals=0, bytes_accessed=4 * cells
        ),
        name="turn_first",
    )(rotation, *blocks)


def advect_turn_kernel(
    pieces, rotation, weights, terms, below, centre, above, low, high, south, north, field, *refs
):
    outs = refs[:pieces]
    mixed, powers = refs[pieces:]
    z = pl.program_id(0)
    last = pl.num_programs(0) - 1
    rows, total, lanes = centre.shape[1:]
    group, count = outs[0].shape[0], outs[0].shape[3]
    pair = 2 if rows % 2 == 0 else 1
    piece = 64 if total % 64 == 0 else total

    def one(step, carry):
        for j in range(pair):
            y = step * pair + j
            powers[...] = jnp.dot(terms[...], field[0, y], preferred_element_type=F32)
            for base in range(0, total, piece):
                part = pl.ds(base, piece)
                f = centre[0, y, part].astype(F32)
                ym = centre[0, jnp.maximum(y - 1, 0), part].astype(F32)
                ym = jnp.where(y == 0, south[0, 0, part].astype(F32), ym)
                yp = centre[0, jnp.minimum(y + 1, rows - 1), part].astype(F32)
                yp = jnp.where(y == rows - 1, north[0, 0, part].astype(F32), yp)
                zm = below[0, y, part].astype(F32)
                zm = jnp.where(z == 0, low[0, y, part].astype(F32), zm)
                zp = above[0, y, part].astype(F32)
                zp = jnp.where(z == last, high[0, y, part].astype(F32), zp)
                moved = weights[6, part] * f
                moved += weights[0, part] * pltpu.roll(f, 1, 1)
                moved += weights[1, part] * pltpu.roll(f, lanes - 1, 1)
                moved += weights[2, part] * ym + weights[3, part] * yp
                moved += weights[4, part] * zm + weights[5, part] * zp
                mixed[part, j * lanes : (j + 1) * lanes] = (
                    moved * jnp.exp(powers[part])
                ).astype(BF16)
        turned = jnp.dot(rotation[...], mixed[...], preferred_element_type=F32)
        span = group * count
        for j in range(pair):
            column = turned[:, j * lanes : (j + 1) * lanes]
            for p in range(pieces):
                mine = column[p * span : (p + 1) * span]
                outs[p][:, 0, step * pair + j] = mine.reshape(group, count, lanes).astype(BF16)
        return carry

    lax.fori_loop(0, rows // pair, one, 0)


def advect_turn(
    rotation, weights, terms, state, low, high, south, north, field, start, owners
):
    depth, rows, total, lanes = state.shape
    count = total // owners
    pieces = block_count(owners)
    group = owners // pieces
    layer = (1, rows, total, lanes)
    edge = (1, 1, total, lanes)
    pair = 2 if rows % 2 == 0 else 1
    cells = total * depth * rows * lanes
    low_last = low.shape[0] - 1
    here = lambda z: (z, 0, 0, 0)
    return pl.pallas_call(
        functools.partial(advect_turn_kernel, pieces),
        grid=(depth,),
        in_specs=[
            pl.BlockSpec((total, total), lambda z: (0, 0)),
            pl.BlockSpec(weights.shape, lambda z: (0, 0, 0)),
            pl.BlockSpec(terms.shape, lambda z: (0, 0)),
            pl.BlockSpec(layer, lambda z: (jnp.maximum(z - 1, 0), 0, 0, 0)),
            pl.BlockSpec(layer, here),
            pl.BlockSpec(layer, lambda z: (jnp.minimum(z + 1, depth - 1), 0, 0, 0)),
            pl.BlockSpec(layer, lambda z: (low_last, 0, 0, 0)),
            pl.BlockSpec(layer, lambda z: (0, 0, 0, 0)),
            pl.BlockSpec(edge, here),
            pl.BlockSpec(edge, here),
            pl.BlockSpec((1,) + field.shape[1:], lambda z: (start + z, 0, 0, 0)),
        ],
        out_specs=[pl.BlockSpec((group, 1, rows, count, lanes), lambda z: (0, z, 0, 0, 0))]
        * pieces,
        out_shape=[jax.ShapeDtypeStruct((group, depth, rows, count, lanes), BF16)] * pieces,
        scratch_shapes=[
            pltpu.VMEM((total, pair * lanes), BF16),
            pltpu.VMEM((total, lanes), F32),
        ],
        cost_estimate=pl.CostEstimate(
            flops=2 * total * cells, transcendentals=cells, bytes_accessed=8 * cells
        ),
        name="advect_turn",
    )(rotation, weights, terms, state, state, state, low, high, south, north, field)


def gather_kernel(pieces, by_owner, coef, place, *refs):
    blocks = refs[:pieces]
    partner = refs[pieces]
    state, partial = refs[-2:]
    group, rows, count = (blocks[0].shape[i] for i in (0, 2, 3))
    base = place[0] if pieces > 1 else None
    kinds = coef.shape[0]
    for index in range(pieces * group):
        part = owner_rows(base, index, rows)
        slot = jnp.bitwise_xor(base, index) if by_owner and pieces > 1 else index
        block = blocks[index // group]
        mine = jnp.swapaxes(block[index % group, 0].astype(F32), 0, 1)
        state[:, 0, part, :] = mine.astype(BF16)
        sums = [None] * kinds
        for o in range(count):
            product = mine[o] * partner[o, 0, part, :].astype(F32)
            for c in range(kinds):
                term = coef[c, o] * product
                sums[c] = term if sums[c] is None else sums[c] + term
        for c in range(kinds):
            partial[slot, c, 0] = sums[c].astype(partial.dtype)


def gather(coef, place, blocks, partner, state, start, closing):
    pieces = len(blocks)
    group, depth, rows, count, lanes = blocks[0].shape
    owners = pieces * group
    kinds = coef.shape[0]
    width = partner.shape[2]
    cells = owners * depth * rows * count * lanes
    slab = pl.BlockSpec((count, 1, width, lanes), lambda z: (0, start + z, 0, 0))
    operands = [coef, place, *blocks, partner]
    in_specs = (
        [pl.BlockSpec(memory_space=pltpu.SMEM)] * 2
        + [pl.BlockSpec((group, 1, rows, count, lanes), lambda z: (0, z, 0, 0, 0))] * pieces
        + [slab]
    )
    aliases = {}
    if state is not None:
        aliases = {len(operands): 0}
        operands.append(state)
        in_specs.append(pl.BlockSpec(memory_space=pl.ANY))
    return pl.pallas_call(
        functools.partial(gather_kernel, pieces, closing),
        grid=(depth,),
        in_specs=in_specs,
        out_specs=[
            slab,
            pl.BlockSpec((owners, kinds, 1, rows, lanes), lambda z: (0, 0, z, 0, 0)),
        ],
        out_shape=[
            jax.ShapeDtypeStruct(partner.shape, BF16),
            jax.ShapeDtypeStruct(
                (owners, kinds, depth, rows, lanes), BF16 if closing else F32
            ),
        ],
        input_output_aliases=aliases,
        cost_estimate=pl.CostEstimate(
            flops=14 * cells, transcendentals=0, bytes_accessed=6 * cells
        ),
        name="gather_last",
    )(*operands)


def swapped(block, distance):
    owners = lax.axis_size("orient")
    return lax.ppermute(block, "orient", [(i, i ^ distance) for i in range(owners)])


def exchange(block):
    return lax.all_to_all(block, "orient", split_axis=0, concat_axis=0, tiled=True)


def exchange_blocks(blocks):
    if len(blocks) == 1:
        return [exchange(blocks[0])]
    came = list(blocks)
    for distance in DISTANCES:
        came[distance] = swapped(blocks[distance], distance)
    return came


def halve(held, narrow):
    stride = 1
    while held.shape[0] > 1:
        half = held.shape[0] // 2
        pairs = held.reshape((half, 2) + held.shape[1:])
        theirs = pairs[:, 1]
        if narrow or half == 1:
            theirs = theirs.astype(BF16)
        came = swapped(theirs, stride)
        held = pairs[:, 0] + came.astype(F32)
        stride *= 2
    return held[0]


def chunk_sizes(layers):
    whole = sum(SHARES)
    sizes = [max(1, layers * share // whole) for share in SHARES]
    sizes[2] += layers - sum(sizes)
    return sizes


def staged_device(q_init, partner, field, orientations, orient_weight, rotation):
    owners = lax.axis_size("orient")
    slabs = lax.axis_size("space")
    me = lax.axis_index("orient")
    count, layers, width, lanes = q_init.shape
    total = rotation.shape[0]
    rows = width // owners
    sizes = chunk_sizes(layers)
    chunks = len(sizes)
    starts = [sum(sizes[:c]) for c in range(chunks)]
    place = me.astype(jnp.int32).reshape(1)

    first = lax.ppermute(q_init[:, layers - 1 :], "space", ring(slabs, 1))
    final = lax.ppermute(q_init[:, :1], "space", ring(slabs, -1))

    field_terms, tensor_terms = angle_tables(orientations)
    weights = stencil_weights(orientations)
    exponent_terms = -step_length * field_terms
    free_terms = jnp.concatenate([tensor_terms[:2], tensor_terms[3:]])
    local_tensor = lax.dynamic_slice_in_dim(
        free_terms * orient_weight[None, :], me * count, count, 1
    )
    wide_weights = jnp.broadcast_to(weights[:, :, None], weights.shape + (lanes,))
    top = lax.reduce_precision(exponent_terms, 8, 7)
    left = exponent_terms - top
    centre = lax.reduce_precision(left, 8, 7)
    split_terms = jnp.concatenate([top, centre, left - centre]).astype(BF16).T
    own_field = lax.dynamic_slice_in_dim(field, me * rows, rows, 2)
    row_field = jnp.transpose(own_field, (1, 2, 0, 3))
    row_field = jnp.concatenate([row_field] * 3, axis=2)
    padding = 32 - split_terms.shape[1]
    split_terms = jnp.pad(split_terms, ((0, 0), (0, padding)))
    row_field = jnp.pad(row_field, ((0, 0), (0, 0), (0, padding), (0, 0)))
    enter = rotation
    leave = rotation
    if paired(owners):
        into = lax.broadcasted_iota(jnp.int32, (total, total), 1)
        source = ((into // count) ^ me) * count + into % count
        chosen = (lax.broadcasted_iota(jnp.int32, (total, total), 0) == source).astype(BF16)
        enter = jnp.dot(rotation, chosen, preferred_element_type=F32).astype(BF16)
        leave = jnp.dot(chosen.T, rotation, preferred_element_type=F32).astype(BF16)

    turned = {}
    souths = {}
    norths = {}
    for c in SENDING:
        sent = advect(
            orientations,
            place,
            q_init,
            first if c == 0 else None,
            final if c == chunks - 1 else None,
            field,
            starts[c],
            sizes[c],
            owners,
        )
        got = exchange_blocks(sent)
        turned[c], top_rows, end_rows = turn(enter, got)
        souths[c] = lax.ppermute(top_rows, "orient", ring(owners, 1))
        norths[c] = lax.ppermute(end_rows, "orient", ring(owners, -1))
    under = lax.ppermute(turned[chunks - 1][-1:], "space", ring(slabs, 1))
    over = lax.ppermute(turned[0][:1], "space", ring(slabs, -1))

    state = None
    sums = {}
    for c in RETURNING:
        sent = advect_turn(
            leave,
            wide_weights,
            split_terms,
            turned[c],
            under if c == 0 else turned[c - 1],
            over if c == chunks - 1 else turned[c + 1],
            souths[c],
            norths[c],
            row_field,
            starts[c],
            owners,
        )
        got = exchange_blocks(sent)
        closing = c in CLOSING or not paired(owners)
        state, partial = gather(
            local_tensor, place, got, partner, state, starts[c], closing
        )
        if closing:
            sums[c] = jnp.sum(exchange(partial).astype(F32), axis=0)
        else:
            sums[c] = halve(partial, c == RETURNING[2])
    free = jnp.concatenate([sums[c] for c in range(chunks)], axis=1)
    tensor = jnp.concatenate([free[:2], -(free[:1] + free[1:2]), free[2:]])
    new_field = (1.0 - relax_rate) * own_field.astype(F32) + relax_rate * coupling * tensor
    return (state, new_field)


def solution(mesh):
    in_specs = (
        P("orient", "space", None, None),
        P("orient", "space", None, None),
        P(None, "space", None, None),
        P(),
        P(),
        P(),
    )
    out_specs = (P("orient", "space", None, None), P(None, "space", "orient", None))
    mapped = jax.shard_map(
        staged_device, mesh=mesh, in_specs=in_specs, out_specs=out_specs, check_vma=False
    )
    if not paired(mesh.shape["orient"]):
        return mapped
    return mapped
```
